512 devices in a mesh: dp: 32 (over z, y_lo, core), ctx: 16 (over y_hi, x).
Axes of the slice: x: 4, y: 8 (y_hi: 4, y_lo: 2; y = y_hi * 2 + y_lo), z: 8, core: 2. Of those that a mesh axis runs over, the one named last changes fastest.
Arguments:
- queries: bfloat16 [32, 2048, 4096], P('dp', 'ctx'), may hold values from -8 to 8
- key_rows: bfloat16 [32, 2048, 512], P('dp', 'ctx'), may hold values from -8 to 8
- values: bfloat16 [32, 2048, 512], P('dp', 'ctx'), may hold values from -6 to 6
- outputs: bfloat16 [32, 2048, 4096], P('dp', 'ctx'), may hold values from -4 to 4
- out_grads: bfloat16 [32, 2048, 4096], P('dp', 'ctx'), may hold values from -6 to 6
- depths: int32 [32, 2048], P('dp', 'ctx'), may hold values from 0 to 63, as said below
- subtree_end: int32 [32, 2048], P('dp', 'ctx'), may hold values from 64 to 2048, as said below
- file_lengths: int32 [32, 8], P('dp'), may hold values from 1 to 1536, 2048 in all within a row
- slopes: float32 [32], replicated, may hold values from 0.02 to 0.5
- ancestor_gain: float32 [32], replicated, may hold values from 0.5 to 3
Outputs:
- query_grads: bfloat16 [32, 2048, 4096], P('dp', 'ctx')
- key_grads: bfloat16 [32, 2048, 512], P('dp', 'ctx')
- value_grads: bfloat16 [32, 2048, 512], P('dp', 'ctx')
- bias_grads: float32 [32, 2], P('ctx')
The draws below stay inside these ranges and needn't reach their ends.
Inputs may be any that keep to these rules, and one draw needn't show every extreme that they name: `depths`: token t has depth t for t < 64; afterwards the depth changes by at most one from a token to the next. `subtree_end`: the first later position of the same sequence whose depth is not above the token's depth, or 2048 where there is none.
All inputs are finite; a program needn't handle non-finite values.
Results may differ from the reference program's by a relative error of at most 0.012.
Values may be sent and summed in bfloat16 or wider, within the bound.
A program may use at most 64 MiB of HBM per device.

```python
import math
import jax
import jax.numpy as jnp
import numpy as np
from jax import lax

QUERY_HEADS = 32
KEY_VALUE_HEADS = 4
HEAD_WIDTH = 128
DEPTHS = 64
FILES = 8
SEQUENCE_LENGTH = 2048
SEQUENCE_COUNT = 32


def drawn_pair(key):
    base_key = jax.random.fold_in(key, 101)
    query_key, key_random_seed = jax.random.split(base_key, 2)
    query_draw = jax.random.normal(query_key, (SEQUENCE_COUNT, SEQUENCE_LENGTH, QUERY_HEADS * HEAD_WIDTH), jnp.float32)
    key_sample = jax.random.normal(key_random_seed, (SEQUENCE_COUNT, SEQUENCE_LENGTH, KEY_VALUE_HEADS * HEAD_WIDTH), jnp.float32)
    return (jnp.clip(query_draw, -8.0, 8.0), jnp.clip(key_sample, -8.0, 8.0))


def draw_queries(key, part):
    return drawn_pair(key)[0].astype(jnp.bfloat16)


def draw_key_rows(key, part):
    return drawn_pair(key)[1].astype(jnp.bfloat16)


def tree_shape(key):
    base_key = jax.random.fold_in(key, 202)
    step_draws = jax.random.randint(base_key, (SEQUENCE_COUNT, SEQUENCE_LENGTH), -1, 2)
    positions = jnp.arange(SEQUENCE_LENGTH, dtype=jnp.int32)

    def advance(current, element):
        step_now, position = element
        following = jnp.where(position < DEPTHS, position, jnp.clip(current + step_now, 0, DEPTHS - 1))
        return (following, following)
    _, walked = lax.scan(advance, jnp.zeros((SEQUENCE_COUNT,), jnp.int32), (step_draws.T, positions))
    depth_rows = walked.T.astype(jnp.int32)

    def subtree_ends(depth_row):
        later = (positions[None, :] > positions[:, None]) & (depth_row[None, :] <= depth_row[:, None])
        return jnp.min(jnp.where(later, positions[None, :], SEQUENCE_LENGTH), axis=1).astype(jnp.int32)
    return (depth_rows, lax.map(subtree_ends, depth_rows))


def draw_depths(key, part):
    return tree_shape(key)[0]


def draw_subtree_end(key, part):
    return tree_shape(key)[1]


def block_levels(own_key, shape, pieces, low, high):
    level = 1.0
    for dim, shards_of in pieces:
        steps = jax.random.uniform(jax.random.fold_in(jax.random.fold_in(own_key, 6), dim), (shards_of,), jnp.float32, low / len(pieces), high / len(pieces))
        level = level * jnp.repeat(jnp.exp(steps), shape[dim] // shards_of).reshape((-1,) + (1,) * (len(shape) - 1 - dim))
    return level


def split_up(amount, total, bound, lean):
    loads = [(1 << 20) // math.isqrt(standing ** lean) + 1 for standing in range(2, amount + 1)]
    spare, counts = total - bound - (amount - 1), [1] * (amount - 1)
    while spare > 0:
        candidates = [i for i in range(amount - 1) if counts[i] < bound]
        pool, remaining = sum([loads[i] for i in candidates]), spare
        for i in candidates:
            more = min(bound - counts[i], max(1, remaining * loads[i] // pool), spare)
            counts[i] = counts[i] + more
            spare = spare - more
    return np.array([bound] + counts)


def uneven(rng, count, total, limit, skew):
    if count == 2:
        one = jax.random.randint(rng, (), max(1, total - limit), min(limit, total - 1) + 1)
        return jnp.stack([one, total - one])
    tallies = jnp.asarray(split_up(count, total, limit, skew), jnp.int32)
    pairs = (count - 1) // 2
    giver, taker = tallies[1:1 + 2 * pairs:2], tallies[2:2 + 2 * pairs:2]
    room = jnp.minimum(giver - 1, limit - taker)
    moved = jax.random.randint(jax.random.fold_in(rng, 1), (pairs,), 0, 1 << 20) % (room + 1)
    tallies = tallies.at[1:1 + 2 * pairs:2].set(giver - moved).at[2:2 + 2 * pairs:2].set(taker + moved)
    return tallies[jax.random.permutation(jax.random.fold_in(rng, 2), count)]


def noise(own_key, dims, width, bound, shards=(), kind=jnp.bfloat16):
    level = block_levels(own_key, dims, shards, -0.22, 0.18) if shards else 1.0
    entries = jax.random.normal(own_key, dims, jnp.float32) * width * level
    return jnp.minimum(jnp.maximum(entries, -bound), bound).astype(kind)


def setup_inputs(seed: int = 0) -> dict:
    streams_of = jax.random.split(jax.random.key(seed), 11)
    return {
        "queries": draw_queries(jax.random.fold_in(streams_of[10], 71), 0),
        "key_rows": draw_key_rows(jax.random.fold_in(streams_of[10], 71), 0),
        "values": noise(streams_of[2], (SEQUENCE_COUNT, SEQUENCE_LENGTH, KEY_VALUE_HEADS * HEAD_WIDTH), 1.0, 6.0, ((0, 32), (1, 16))),
        "outputs": noise(streams_of[3], (SEQUENCE_COUNT, SEQUENCE_LENGTH, QUERY_HEADS * HEAD_WIDTH), 0.5, 4.0, ((0, 32), (1, 16))),
        "out_grads": noise(streams_of[4], (SEQUENCE_COUNT, SEQUENCE_LENGTH, QUERY_HEADS * HEAD_WIDTH), 1.0, 6.0, ((0, 32), (1, 16))),
        "depths": draw_depths(jax.random.fold_in(streams_of[10], 71), 0),
        "subtree_end": draw_subtree_end(jax.random.fold_in(streams_of[10], 71), 0),
        "file_lengths": jax.vmap(lambda own: uneven(own, FILES, SEQUENCE_LENGTH, SEQUENCE_LENGTH * 3 // 4, 2))(jax.random.split(streams_of[7], SEQUENCE_COUNT)).reshape((SEQUENCE_COUNT, FILES)).astype(jnp.int32),
        "slopes": jnp.clip(jnp.exp(jax.random.uniform(streams_of[8], (QUERY_HEADS,), jnp.float32, math.log(0.02), math.log(0.5))), 0.02, 0.5),
        "ancestor_gain": jnp.clip(jax.random.uniform(streams_of[9], (QUERY_HEADS,), jnp.float32, 0.5, 3.0), 0.5, 3.0),
    }


masked_score = -1.0e30


def head_terms(query_h, key_h, value_h, output_h, grad_h, slope_h, gain_h, distance, ancestor, allowed):
    factor = HEAD_WIDTH ** -0.5
    scores = jnp.dot(query_h, key_h.T, preferred_element_type=jnp.float32) * factor
    scores = scores - slope_h * distance + gain_h * ancestor
    scores = jnp.where(allowed, scores, masked_score)
    row_top = jnp.max(scores, axis=1, keepdims=True)
    log_total = row_top + jnp.log(jnp.sum(jnp.exp(scores - row_top), axis=1, keepdims=True))
    probs = jnp.exp(scores - log_total)
    probs_b = probs.astype(jnp.bfloat16)
    row_delta = jnp.sum(grad_h.astype(jnp.float32) * output_h.astype(jnp.float32), axis=1, keepdims=True)
    dprobs = jnp.dot(grad_h, value_h.T, preferred_element_type=jnp.float32)
    dscores = probs * (dprobs - row_delta)
    dscores_b = dscores.astype(jnp.bfloat16)
    query_g = (jnp.dot(dscores_b, key_h, preferred_element_type=jnp.float32) * factor).astype(jnp.bfloat16)
    key_gradient = jnp.dot(dscores_b.T, query_h, preferred_element_type=jnp.float32) * factor
    value_gradient = jnp.dot(probs_b.T, grad_h, preferred_element_type=jnp.float32)
    slope_g = -jnp.sum(dscores * distance)
    gain_g = jnp.sum(dscores * ancestor)
    return query_g, key_gradient, value_gradient, jnp.stack([slope_g, gain_g])


def reference(queries, key_rows, values, outputs, out_grads, depths, subtree_end, file_lengths, slopes, ancestor_gain):
    positions = jnp.arange(SEQUENCE_LENGTH, dtype=jnp.int32)
    group_width = QUERY_HEADS // KEY_VALUE_HEADS

    def one_sequence(inputs):
        query_s, key_sequence, value_sequence, output_s, grad_s, depth_s, end_s, length_s = inputs
        bounds = jnp.cumsum(length_s)
        file_id = jnp.sum((positions[:, None] >= bounds[None, :]).astype(jnp.int32), axis=1)
        earlier = positions[None, :] <= positions[:, None]
        allowed = earlier & (file_id[:, None] == file_id[None, :])
        ancestor = (earlier & (positions[:, None] < end_s[None, :])).astype(jnp.float32)
        distance = jnp.abs(depth_s[:, None] - depth_s[None, :]).astype(jnp.float32)
        query_three = query_s.reshape(SEQUENCE_LENGTH, QUERY_HEADS, HEAD_WIDTH)
        output_three = output_s.reshape(SEQUENCE_LENGTH, QUERY_HEADS, HEAD_WIDTH)
        grad_three = grad_s.reshape(SEQUENCE_LENGTH, QUERY_HEADS, HEAD_WIDTH)
        key_triple = key_sequence.reshape(SEQUENCE_LENGTH, KEY_VALUE_HEADS, HEAD_WIDTH)
        value_triple = value_sequence.reshape(SEQUENCE_LENGTH, KEY_VALUE_HEADS, HEAD_WIDTH)

        def one_head(head_index):
            kv_index = head_index // group_width
            query_h = lax.dynamic_index_in_dim(query_three, head_index, 1, False)
            output_h = lax.dynamic_index_in_dim(output_three, head_index, 1, False)
            grad_h = lax.dynamic_index_in_dim(grad_three, head_index, 1, False)
            key_h = lax.dynamic_index_in_dim(key_triple, kv_index, 1, False)
            value_h = lax.dynamic_index_in_dim(value_triple, kv_index, 1, False)
            slope_h = lax.dynamic_index_in_dim(slopes, head_index, 0, False)
            gain_h = lax.dynamic_index_in_dim(ancestor_gain, head_index, 0, False)
            return head_terms(query_h, key_h, value_h, output_h, grad_h, slope_h, gain_h, distance, ancestor, allowed)

        query_g, key_gradient, value_gradient, bias_g = lax.map(one_head, jnp.arange(QUERY_HEADS, dtype=jnp.int32))
        query_out = jnp.transpose(query_g, (1, 0, 2)).reshape(SEQUENCE_LENGTH, QUERY_HEADS * HEAD_WIDTH)
        key_total_sum = jnp.sum(key_gradient.reshape(KEY_VALUE_HEADS, group_width, SEQUENCE_LENGTH, HEAD_WIDTH), axis=1)
        value_total_sum = jnp.sum(value_gradient.reshape(KEY_VALUE_HEADS, group_width, SEQUENCE_LENGTH, HEAD_WIDTH), axis=1)
        key_result = jnp.transpose(key_total_sum, (1, 0, 2)).reshape(SEQUENCE_LENGTH, KEY_VALUE_HEADS * HEAD_WIDTH).astype(jnp.bfloat16)
        value_result = jnp.transpose(value_total_sum, (1, 0, 2)).reshape(SEQUENCE_LENGTH, KEY_VALUE_HEADS * HEAD_WIDTH).astype(jnp.bfloat16)
        return query_out, key_result, value_result, bias_g

    results = lax.map(one_sequence, (queries, key_rows, values, outputs, out_grads, depths, subtree_end, file_lengths))
    return results[0], results[1], results[2], jnp.sum(results[3], axis=0)
```

```python
import functools

import jax
import jax.numpy as jnp
from jax import lax
from jax.experimental import pallas as pl
from jax.experimental.pallas import tpu as pltpu
from jax.sharding import PartitionSpec as P

HEAD_WIDTH = 128
BLOCK = 256

masked_score = -1e30


def _grads_kernel(
    lo_ref,
    sg_ref,
    q_ref,
    qT_ref,
    do_ref,
    doT_ref,
    delta_ref,
    k_ref,
    kT_ref,
    vT_ref,
    dcol_ref,
    fcol_ref,
    drow_ref,
    frow_ref,
    erow_ref,
    dq_ref,
    dkT_ref,
    dvT_ref,
    bias_ref,
    s_scr,
    m_scr,
    l_scr,
    dq_scr,
    *,
    nh,
    hw,
    bq,
    bk,
    factor,
):
    i = pl.program_id(0)

    @pl.when(i == 0)
    def _():
        dkT_ref[...] = jnp.zeros_like(dkT_ref)
        dvT_ref[...] = jnp.zeros_like(dvT_ref)
        bias_ref[...] = jnp.zeros_like(bias_ref)

    q0 = i * bq
    lo = lo_ref[i]
    qpos = q0 + lax.broadcasted_iota(jnp.int32, (bq, 1), 0)
    dcol = dcol_ref[...]
    fcol = fcol_ref[...]

    def tile_masks(kb):
        k0 = pl.multiple_of(kb * bk, bk)
        kpos = k0 + lax.broadcasted_iota(jnp.int32, (1, bk), 1)
        drow = drow_ref[:, pl.ds(k0, bk)]
        frow = frow_ref[:, pl.ds(k0, bk)]
        erow = erow_ref[:, pl.ds(k0, bk)]
        causal = kpos <= qpos
        allowed = causal & (fcol == frow)
        anc = jnp.where(causal & (qpos < erow), 1.0, 0.0).astype(jnp.float32)
        dist = jnp.abs(dcol - drow).astype(jnp.float32)
        return k0, allowed, anc, dist

    m_scr[...] = jnp.full(m_scr.shape, masked_score, jnp.float32)
    l_scr[...] = jnp.zeros(l_scr.shape, jnp.float32)

    def stats(kb, carry):
        k0, allowed, anc, dist = tile_masks(kb)
        kT = kT_ref[:, pl.ds(k0, bk)]
        for h in range(nh):
            raw = jnp.dot(q_ref[:, h * hw : (h + 1) * hw], kT, preferred_element_type=jnp.float32)
            s = raw * factor
            s = s - sg_ref[h] * dist + sg_ref[nh + h] * anc
            s = jnp.where(allowed, s, masked_score)
            s_scr[h, kb] = s
            m_old = m_scr[h]
            m_new = jnp.maximum(m_old, jnp.max(s, axis=1, keepdims=True))
            l_scr[h] = l_scr[h] * jnp.exp(m_old - m_new) + jnp.sum(
                jnp.exp(s - m_new), axis=1, keepdims=True
            )
            m_scr[h] = m_new
        return carry

    lax.fori_loop(lo, i + 1, stats, 0)
    for h in range(nh):
        m_scr[h] = m_scr[h] + jnp.log(l_scr[h])
    dq_scr[...] = jnp.zeros(dq_scr.shape, jnp.float32)

    def grads(kb, carry):
        k0, _, anc, dist = tile_masks(kb)
        vT = vT_ref[:, pl.ds(k0, bk)]
        kblk = k_ref[pl.ds(k0, bk), :]
        for h in range(nh):
            s = s_scr[h, kb]
            p = jnp.exp(s - m_scr[h])
            dp = jnp.dot(do_ref[:, h * hw : (h + 1) * hw], vT, preferred_element_type=jnp.float32)
            ds = p * (dp - delta_ref[:, h : h + 1])
            ds_b = ds.astype(jnp.bfloat16)
            p_b = p.astype(jnp.bfloat16)
            dq_scr[h] += jnp.dot(ds_b, kblk, preferred_element_type=jnp.float32)
            dkT_ref[:, pl.ds(k0, bk)] += jnp.dot(
                qT_ref[h * hw : (h + 1) * hw, :], ds_b, preferred_element_type=jnp.float32
            )
            dvT_ref[:, pl.ds(k0, bk)] += jnp.dot(
                doT_ref[h * hw : (h + 1) * hw, :], p_b, preferred_element_type=jnp.float32
            )
            bias_ref[h] += jnp.sum(ds * dist, axis=0, keepdims=True)
            bias_ref[nh + h] += jnp.sum(ds * anc, axis=0, keepdims=True)
        return carry

    lax.fori_loop(lo, i + 1, grads, 0)
    for h in range(nh):
        dq_ref[:, h * hw : (h + 1) * hw] = (dq_scr[h] * factor).astype(dq_ref.dtype)


def attention_grads(q, qT, do, doT, delta, k, kT, vT, dcol, fcol, drow, frow, erow, lo, sg, interpret=False):
    seq_len, width = q.shape
    hw = k.shape[1]
    nh = width // hw
    bq = bk = min(BLOCK, seq_len)
    nq = seq_len // bq
    nk = seq_len // bk
    factor = hw ** (-0.5)
    kernel = functools.partial(_grads_kernel, nh=nh, hw=hw, bq=bq, bk=bk, factor=factor)
    full = lambda shape: pl.BlockSpec(shape, lambda i, lo: (0,) * len(shape))
    grid_spec = pltpu.PrefetchScalarGridSpec(
        num_scalar_prefetch=1,
        grid=(nq,),
        in_specs=[
            pl.BlockSpec(memory_space=pltpu.SMEM),
            pl.BlockSpec((bq, width), lambda i, lo: (i, 0)),
            pl.BlockSpec((width, bq), lambda i, lo: (0, i)),
            pl.BlockSpec((bq, width), lambda i, lo: (i, 0)),
            pl.BlockSpec((width, bq), lambda i, lo: (0, i)),
            pl.BlockSpec((bq, nh), lambda i, lo: (i, 0)),
            full((seq_len, hw)),
            full((hw, seq_len)),
            full((hw, seq_len)),
            pl.BlockSpec((bq, 1), lambda i, lo: (i, 0)),
            pl.BlockSpec((bq, 1), lambda i, lo: (i, 0)),
            full((1, seq_len)),
            full((1, seq_len)),
            full((1, seq_len)),
        ],
        out_specs=[
            pl.BlockSpec((bq, width), lambda i, lo: (i, 0)),
            full((hw, seq_len)),
            full((hw, seq_len)),
            full((2 * nh, 1, bk)),
        ],
        scratch_shapes=[
            pltpu.VMEM((nh, nk, bq, bk), jnp.float32),
            pltpu.VMEM((nh, bq, 1), jnp.float32),
            pltpu.VMEM((nh, bq, 1), jnp.float32),
            pltpu.VMEM((nh, bq, hw), jnp.float32),
        ],
    )
    causal_tiles = nq * (nq + 1) // 2
    flops = 2 * 5 * nh * causal_tiles * bq * bk * hw
    return pl.pallas_call(
        kernel,
        grid_spec=grid_spec,
        out_shape=[
            jax.ShapeDtypeStruct((seq_len, width), jnp.bfloat16),
            jax.ShapeDtypeStruct((hw, seq_len), jnp.float32),
            jax.ShapeDtypeStruct((hw, seq_len), jnp.float32),
            jax.ShapeDtypeStruct((2 * nh, 1, bk), jnp.float32),
        ],
        compiler_params=pltpu.CompilerParams(
            dimension_semantics=("arbitrary",), vmem_limit_bytes=48 * 1024 * 1024
        ),
        cost_estimate=pl.CostEstimate(
            flops=flops,
            transcendentals=2 * nh * causal_tiles * bq * bk,
            bytes_accessed=8 * seq_len * width + 8 * seq_len * hw,
        ),
        interpret=interpret,
    )(lo, sg, q, qT, do, doT, delta, k, kT, vT, dcol, fcol, drow, frow, erow)


def body(
    queries,
    key_rows,
    values,
    outputs,
    out_grads,
    depths,
    subtree_end,
    file_lengths,
    slopes,
    ancestor_gain,
):
    tokens_here = queries.shape[1]
    context_size = lax.axis_size("ctx")
    heads_all = queries.shape[2] // HEAD_WIDTH
    kv_heads = key_rows.shape[2] // HEAD_WIDTH
    local_heads = heads_all // context_size
    group_width = heads_all // kv_heads
    repeats = context_size // kv_heads
    assert group_width // local_heads == repeats
    seq_len = tokens_here * context_size
    block = min(BLOCK, seq_len)
    factor = HEAD_WIDTH ** (-0.5)
    head_first = lax.axis_index("ctx") * local_heads
    local_slopes = lax.dynamic_slice_in_dim(slopes, head_first, local_heads)
    local_gains = lax.dynamic_slice_in_dim(ancestor_gain, head_first, local_heads)
    sg = jnp.concatenate([local_slopes, local_gains])
    depth_whole = lax.all_gather(depths[0], "ctx", axis=0, tiled=True)
    end_whole = lax.all_gather(subtree_end[0], "ctx", axis=0, tiled=True)
    positions = jnp.arange(seq_len, dtype=jnp.int32)
    lengths = file_lengths[0]
    bounds = jnp.cumsum(lengths)
    starts = bounds - lengths
    file_whole = jnp.sum((positions[:, None] >= bounds[None, :]).astype(jnp.int32), axis=1)
    file_start = starts[jnp.minimum(file_whole, lengths.shape[0] - 1)]
    lo = (file_start[::block] // block).astype(jnp.int32)

    delta_tok = jnp.sum(
        (out_grads[0].astype(jnp.float32) * outputs[0].astype(jnp.float32)).reshape(
            tokens_here, heads_all, HEAD_WIDTH
        ),
        axis=2,
    )
    delta_heads = lax.all_to_all(
        delta_tok.reshape(tokens_here, context_size, local_heads), "ctx", split_axis=1, concat_axis=0, tiled=True
    ).reshape(seq_len, local_heads)
    query_split = queries[0].reshape(tokens_here, context_size, local_heads * HEAD_WIDTH)
    grad_split = out_grads[0].reshape(tokens_here, context_size, local_heads * HEAD_WIDTH)
    query_heads = lax.all_to_all(query_split, "ctx", split_axis=1, concat_axis=0, tiled=True)
    grad_heads = lax.all_to_all(grad_split, "ctx", split_axis=1, concat_axis=0, tiled=True)
    query_heads = query_heads.reshape(seq_len, local_heads * HEAD_WIDTH)
    grad_heads = grad_heads.reshape(seq_len, local_heads * HEAD_WIDTH)
    key_rep = jnp.repeat(key_rows[0].reshape(tokens_here, kv_heads, HEAD_WIDTH), repeats, axis=1)
    value_rep = jnp.repeat(values[0].reshape(tokens_here, kv_heads, HEAD_WIDTH), repeats, axis=1)
    key_head = lax.all_to_all(key_rep, "ctx", split_axis=1, concat_axis=0, tiled=True).reshape(seq_len, HEAD_WIDTH)
    value_head = lax.all_to_all(value_rep, "ctx", split_axis=1, concat_axis=0, tiled=True).reshape(
        seq_len, HEAD_WIDTH
    )

    dq, dkT, dvT, bias_part = attention_grads(
        query_heads,
        query_heads.T,
        grad_heads,
        grad_heads.T,
        delta_heads,
        key_head,
        key_head.T,
        value_head.T,
        depth_whole[:, None],
        file_whole[:, None],
        depth_whole[None, :],
        file_whole[None, :],
        end_whole[None, :],
        lo,
        sg,
    )

    query_back = lax.all_to_all(
        dq.reshape(seq_len, 1, local_heads * HEAD_WIDTH), "ctx", split_axis=0, concat_axis=1, tiled=True
    )
    query_grads = query_back.reshape(1, tokens_here, heads_all * HEAD_WIDTH)
    key_scaled = (dkT.T * factor).reshape(seq_len, 1, HEAD_WIDTH)
    value_scaled = dvT.T.reshape(seq_len, 1, HEAD_WIDTH)
    key_back = lax.all_to_all(
        key_scaled.astype(jnp.bfloat16), "ctx", split_axis=0, concat_axis=1, tiled=True
    ).astype(jnp.float32)
    value_back = lax.all_to_all(
        value_scaled.astype(jnp.bfloat16), "ctx", split_axis=0, concat_axis=1, tiled=True
    ).astype(jnp.float32)
    key_grads = jnp.sum(key_back.reshape(tokens_here, kv_heads, repeats, HEAD_WIDTH), axis=2)
    value_grads = jnp.sum(value_back.reshape(tokens_here, kv_heads, repeats, HEAD_WIDTH), axis=2)
    key_grads = key_grads.astype(jnp.bfloat16).reshape(1, tokens_here, kv_heads * HEAD_WIDTH)
    value_grads = value_grads.astype(jnp.bfloat16).reshape(1, tokens_here, kv_heads * HEAD_WIDTH)
    bias_sums = jnp.sum(bias_part, axis=(1, 2))
    bias_local = jnp.stack([-bias_sums[:local_heads], bias_sums[local_heads:]], axis=1)
    bias_grads = lax.psum(bias_local, "dp")
    return (query_grads, key_grads, value_grads, bias_grads)


def solution(mesh):
    in_specs = (
        P("dp", "ctx", None),
        P("dp", "ctx", None),
        P("dp", "ctx", None),
        P("dp", "ctx", None),
        P("dp", "ctx", None),
        P("dp", "ctx"),
        P("dp", "ctx"),
        P("dp", None),
        P(),
        P(),
    )
    out_specs = (P("dp", "ctx", None), P("dp", "ctx", None), P("dp", "ctx", None), P("ctx", None))
    return jax.shard_map(body, mesh=mesh, in_specs=in_specs, out_specs=out_specs, check_vma=False)
```

```python
import functools

import jax
import jax.numpy as jnp
from jax import lax
from jax.experimental import pallas as pl
from jax.experimental.pallas import tpu as pltpu
from jax.sharding import PartitionSpec as P

HEAD_WIDTH = 128
BLOCK = 256

masked_score = -1e30


def _grads_kernel(
    lo_ref,
    sg_ref,
    q_ref,
    qT_ref,
    do_ref,
    doT_ref,
    delta_ref,
    k_ref,
    kT_ref,
    vT_ref,
    dcol_ref,
    fcol_ref,
    drow_ref,
    frow_ref,
    erow_ref,
    dq_ref,
    dkT_ref,
    dvT_ref,
    bias_ref,
    s_scr,
    m_scr,
    l_scr,
    dq_scr,
    *,
    nh,
    hw,
    bq,
    bk,
    factor,
):
    i = pl.program_id(0)

    @pl.when(i == 0)
    def _():
        dkT_ref[...] = jnp.zeros_like(dkT_ref)
        dvT_ref[...] = jnp.zeros_like(dvT_ref)
        bias_ref[...] = jnp.zeros_like(bias_ref)

    q0 = i * bq
    lo = lo_ref[i]
    qpos = q0 + lax.broadcasted_iota(jnp.int32, (bq, 1), 0)
    dcol = dcol_ref[...]
    fcol = fcol_ref[...]

    def tile_masks(kb):
        k0 = pl.multiple_of(kb * bk, bk)
        kpos = k0 + lax.broadcasted_iota(jnp.int32, (1, bk), 1)
        drow = drow_ref[:, pl.ds(k0, bk)]
        frow = frow_ref[:, pl.ds(k0, bk)]
        erow = erow_ref[:, pl.ds(k0, bk)]
        causal = kpos <= qpos
        allowed = causal & (fcol == frow)
        anc = jnp.where(causal & (qpos < erow), 1.0, 0.0).astype(jnp.float32)
        dist = jnp.abs(dcol - drow).astype(jnp.float32)
        return k0, allowed, anc, dist

    m_scr[...] = jnp.full(m_scr.shape, masked_score, jnp.float32)
    l_scr[...] = jnp.zeros(l_scr.shape, jnp.float32)

    def stats(kb, carry):
        k0, allowed, anc, dist = tile_masks(kb)
        kT = kT_ref[:, pl.ds(k0, bk)]
        for h in range(nh):
            raw = jnp.dot(q_ref[:, h * hw : (h + 1) * hw], kT, preferred_element_type=jnp.float32)
            s = raw * factor
            s = s - sg_ref[h] * dist + sg_ref[nh + h] * anc
            s = jnp.where(allowed, s, masked_score)
            s_scr[h, kb] = s
            m_old = m_scr[h]
            m_new = jnp.maximum(m_old, jnp.max(s, axis=1, keepdims=True))
            l_scr[h] = l_scr[h] * jnp.exp(m_old - m_new) + jnp.sum(
                jnp.exp(s - m_new), axis=1, keepdims=True
            )
            m_scr[h] = m_new
        return carry

    lax.fori_loop(lo, i + 1, stats, 0)
    for h in range(nh):
        m_scr[h] = m_scr[h] + jnp.log(l_scr[h])
    dq_scr[...] = jnp.zeros(dq_scr.shape, jnp.float32)

    def grads(kb, carry):
        k0, _, anc, dist = tile_masks(kb)
        vT = vT_ref[:, pl.ds(k0, bk)]
        kblk = k_ref[pl.ds(k0, bk), :]
        for h in range(nh):
            s = s_scr[h, kb]
            p = jnp.exp(s - m_scr[h])
            dp = jnp.dot(do_ref[:, h * hw : (h + 1) * hw], vT, preferred_element_type=jnp.float32)
            ds = p * (dp - delta_ref[:, h : h + 1])
            ds_b = ds.astype(jnp.bfloat16)
            p_b = p.astype(jnp.bfloat16)
            dq_scr[h] += jnp.dot(ds_b, kblk, preferred_element_type=jnp.float32)
            dkT_ref[:, pl.ds(k0, bk)] += jnp.dot(
                qT_ref[h * hw : (h + 1) * hw, :], ds_b, preferred_element_type=jnp.float32
            )
            dvT_ref[:, pl.ds(k0, bk)] += jnp.dot(
                doT_ref[h * hw : (h + 1) * hw, :], p_b, preferred_element_type=jnp.float32
            )
            bias_ref[h] += jnp.sum(ds * dist, axis=0, keepdims=True)
            bias_ref[nh + h] += jnp.sum(ds * anc, axis=0, keepdims=True)
        return carry

    lax.fori_loop(lo, i + 1, grads, 0)
    for h in range(nh):
        dq_ref[:, h * hw : (h + 1) * hw] = (dq_scr[h] * factor).astype(dq_ref.dtype)


def attention_grads(q, qT, do, doT, delta, k, kT, vT, dcol, fcol, drow, frow, erow, lo, sg, interpret=False):
    seq_len, width = q.shape
    hw = k.shape[1]
    nh = width // hw
    bq = bk = min(BLOCK, seq_len)
    nq = seq_len // bq
    nk = seq_len // bk
    factor = hw ** (-0.5)
    kernel = functools.partial(_grads_kernel, nh=nh, hw=hw, bq=bq, bk=bk, factor=factor)
    full = lambda shape: pl.BlockSpec(shape, lambda i, lo: (0,) * len(shape))
    grid_spec = pltpu.PrefetchScalarGridSpec(
        num_scalar_prefetch=1,
        grid=(nq,),
        in_specs=[
            pl.BlockSpec(memory_space=pltpu.SMEM),
            pl.BlockSpec((bq, width), lambda i, lo: (i, 0)),
            pl.BlockSpec((width, bq), lambda i, lo: (0, i)),
            pl.BlockSpec((bq, width), lambda i, lo: (i, 0)),
            pl.BlockSpec((width, bq), lambda i, lo: (0, i)),
            pl.BlockSpec((bq, nh), lambda i, lo: (i, 0)),
            full((seq_len, hw)),
            full((hw, seq_len)),
            full((hw, seq_len)),
            pl.BlockSpec((bq, 1), lambda i, lo: (i, 0)),
            pl.BlockSpec((bq, 1), lambda i, lo: (i, 0)),
            full((1, seq_len)),
            full((1, seq_len)),
            full((1, seq_len)),
        ],
        out_specs=[
            pl.BlockSpec((bq, width), lambda i, lo: (i, 0)),
            full((hw, seq_len)),
            full((hw, seq_len)),
            full((2 * nh, 1, bk)),
        ],
        scratch_shapes=[
            pltpu.VMEM((nh, nk, bq, bk), jnp.float32),
            pltpu.VMEM((nh, bq, 1), jnp.float32),
            pltpu.VMEM((nh, bq, 1), jnp.float32),
            pltpu.VMEM((nh, bq, hw), jnp.float32),
        ],
    )
    causal_tiles = nq * (nq + 1) // 2
    flops = 2 * 5 * nh * causal_tiles * bq * bk * hw
    return pl.pallas_call(
        kernel,
        grid_spec=grid_spec,
        out_shape=[
            jax.ShapeDtypeStruct((seq_len, width), jnp.bfloat16),
            jax.ShapeDtypeStruct((hw, seq_len), jnp.float32),
            jax.ShapeDtypeStruct((hw, seq_len), jnp.float32),
            jax.ShapeDtypeStruct((2 * nh, 1, bk), jnp.float32),
        ],
        compiler_params=pltpu.CompilerParams(
            dimension_semantics=("arbitrary",), vmem_limit_bytes=48 * 1024 * 1024
        ),
        cost_estimate=pl.CostEstimate(
            flops=flops,
            transcendentals=2 * nh * causal_tiles * bq * bk,
            bytes_accessed=8 * seq_len * width + 8 * seq_len * hw,
        ),
        interpret=interpret,
    )(lo, sg, q, qT, do, doT, delta, k, kT, vT, dcol, fcol, drow, frow, erow)


def body(
    queries,
    key_rows,
    values,
    outputs,
    out_grads,
    depths,
    subtree_end,
    file_lengths,
    slopes,
    ancestor_gain,
):
    tokens_here = queries.shape[1]
    context_size = lax.axis_size("ctx")
    heads_all = queries.shape[2] // HEAD_WIDTH
    kv_heads = key_rows.shape[2] // HEAD_WIDTH
    local_heads = heads_all // context_size
    group_width = heads_all // kv_heads
    repeats = context_size // kv_heads
    assert group_width // local_heads == repeats
    seq_len = tokens_here * context_size
    block = min(BLOCK, seq_len)
    factor = HEAD_WIDTH ** (-0.5)
    head_first = lax.axis_index("ctx") * local_heads
    local_slopes = lax.dynamic_slice_in_dim(slopes, head_first, local_heads)
    local_gains = lax.dynamic_slice_in_dim(ancestor_gain, head_first, local_heads)
    sg = jnp.concatenate([local_slopes, local_gains])
    positions = jnp.arange(seq_len, dtype=jnp.int32)
    lengths = file_lengths[0]
    bounds = jnp.cumsum(lengths)
    starts = bounds - lengths
    file_whole = jnp.sum((positions[:, None] >= bounds[None, :]).astype(jnp.int32), axis=1)
    file_start = starts[jnp.minimum(file_whole, lengths.shape[0] - 1)]
    lo = (file_start[::block] // block).astype(jnp.int32)

    delta_tok = jnp.sum(
        (out_grads[0].astype(jnp.float32) * outputs[0].astype(jnp.float32)).reshape(
            tokens_here, heads_all, HEAD_WIDTH
        ),
        axis=2,
    )
    tree_tok = jnp.stack([depths[0], subtree_end[0]], axis=1).astype(jnp.float32)
    small_pack = jnp.concatenate(
        [
            delta_tok.reshape(tokens_here, context_size, local_heads),
            jnp.broadcast_to(tree_tok[:, None, :], (tokens_here, context_size, 2)),
        ],
        axis=2,
    )
    small_heads = lax.all_to_all(small_pack, "ctx", split_axis=1, concat_axis=0, tiled=True).reshape(
        seq_len, local_heads + 2
    )
    delta_heads = small_heads[:, :local_heads]
    depth_whole = small_heads[:, local_heads].astype(jnp.int32)
    end_whole = small_heads[:, local_heads + 1].astype(jnp.int32)

    width = local_heads * HEAD_WIDTH
    big_pack = jnp.concatenate(
        [
            queries[0].reshape(tokens_here, context_size, width),
            out_grads[0].reshape(tokens_here, context_size, width),
            jnp.repeat(key_rows[0].reshape(tokens_here, kv_heads, HEAD_WIDTH), repeats, axis=1),
            jnp.repeat(values[0].reshape(tokens_here, kv_heads, HEAD_WIDTH), repeats, axis=1),
        ],
        axis=2,
    )
    big_heads = lax.all_to_all(big_pack, "ctx", split_axis=1, concat_axis=0, tiled=True).reshape(
        seq_len, 2 * width + 2 * HEAD_WIDTH
    )
    query_heads = big_heads[:, :width]
    grad_heads = big_heads[:, width : 2 * width]
    key_head = big_heads[:, 2 * width : 2 * width + HEAD_WIDTH]
    value_head = big_heads[:, 2 * width + HEAD_WIDTH :]

    dq, dkT, dvT, bias_part = attention_grads(
        query_heads,
        query_heads.T,
        grad_heads,
        grad_heads.T,
        delta_heads,
        key_head,
        key_head.T,
        value_head.T,
        depth_whole[:, None],
        file_whole[:, None],
        depth_whole[None, :],
        file_whole[None, :],
        end_whole[None, :],
        lo,
        sg,
    )

    back_pack = jnp.concatenate(
        [dq, (dkT.T * factor).astype(jnp.bfloat16), dvT.T.astype(jnp.bfloat16)], axis=1
    ).reshape(seq_len, 1, width + 2 * HEAD_WIDTH)
    back = lax.all_to_all(back_pack, "ctx", split_axis=0, concat_axis=1, tiled=True)
    query_grads = back[:, :, :width].reshape(1, tokens_here, heads_all * HEAD_WIDTH)
    key_back = back[:, :, width : width + HEAD_WIDTH].astype(jnp.float32)
    value_back = back[:, :, width + HEAD_WIDTH :].astype(jnp.float32)
    key_grads = jnp.sum(key_back.reshape(tokens_here, kv_heads, repeats, HEAD_WIDTH), axis=2)
    value_grads = jnp.sum(value_back.reshape(tokens_here, kv_heads, repeats, HEAD_WIDTH), axis=2)
    key_grads = key_grads.astype(jnp.bfloat16).reshape(1, tokens_here, kv_heads * HEAD_WIDTH)
    value_grads = value_grads.astype(jnp.bfloat16).reshape(1, tokens_here, kv_heads * HEAD_WIDTH)
    bias_sums = jnp.sum(bias_part, axis=(1, 2))
    bias_local = jnp.stack([-bias_sums[:local_heads], bias_sums[local_heads:]], axis=1)
    bias_slots = lax.dynamic_update_slice_in_dim(
        jnp.zeros((heads_all, 2), jnp.float32), bias_local, head_first, 0
    )
    bias_total = lax.psum(bias_slots, ("dp", "ctx"))
    bias_grads = lax.dynamic_slice_in_dim(bias_total, head_first, local_heads, 0)
    return (query_grads, key_grads, value_grads, bias_grads)


def solution(mesh):
    in_specs = (
        P("dp", "ctx", None),
        P("dp", "ctx", None),
        P("dp", "ctx", None),
        P("dp", "ctx", None),
        P("dp", "ctx", None),
        P("dp", "ctx"),
        P("dp", "ctx"),
        P("dp", None),
        P(),
        P(),
    )
    out_specs = (P("dp", "ctx", None), P("dp", "ctx", None), P("dp", "ctx", None), P("ctx", None))
    return jax.shard_map(body, mesh=mesh, in_specs=in_specs, out_specs=out_specs, check_vma=False)
```

```python
import functools

import jax
import jax.numpy as jnp
from jax import lax
from jax.experimental import pallas as pl
from jax.experimental.pallas import tpu as pltpu
from jax.sharding import PartitionSpec as P

HEAD_WIDTH = 128
BLOCK = 256

masked_score = -1e30


def _grads_kernel(
    lo_ref,
    sg_ref,
    q_ref,
    qT_ref,
    do_ref,
    doT_ref,
    delta_ref,
    k_ref,
    kT_ref,
    vT_ref,
    dcol_ref,
    fcol_ref,
    drow_ref,
    frow_ref,
    erow_ref,
    dq_ref,
    dkT_ref,
    dvT_ref,
    bias_ref,
    s_scr,
    m_scr,
    l_scr,
    dq_scr,
    *,
    nh,
    hw,
    bq,
    bk,
    factor,
):
    i = pl.program_id(0)

    @pl.when(i == 0)
    def _():
        dkT_ref[...] = jnp.zeros_like(dkT_ref)
        dvT_ref[...] = jnp.zeros_like(dvT_ref)
        bias_ref[...] = jnp.zeros_like(bias_ref)

    q0 = i * bq
    lo = lo_ref[i]
    qpos = q0 + lax.broadcasted_iota(jnp.int32, (bq, 1), 0)
    dcol = dcol_ref[...]
    fcol = fcol_ref[...]

    def tile_masks(kb):
        k0 = pl.multiple_of(kb * bk, bk)
        kpos = k0 + lax.broadcasted_iota(jnp.int32, (1, bk), 1)
        drow = drow_ref[:, pl.ds(k0, bk)]
        frow = frow_ref[:, pl.ds(k0, bk)]
        erow = erow_ref[:, pl.ds(k0, bk)]
        causal = kpos <= qpos
        allowed = causal & (fcol == frow)
        anc = jnp.where(causal & (qpos < erow), 1.0, 0.0).astype(jnp.float32)
        dist = jnp.abs(dcol - drow).astype(jnp.float32)
        return k0, allowed, anc, dist

    m_scr[...] = jnp.full(m_scr.shape, masked_score, jnp.float32)
    l_scr[...] = jnp.zeros(l_scr.shape, jnp.float32)

    def stats(kb, carry):
        k0, allowed, anc, dist = tile_masks(kb)
        kT = kT_ref[:, pl.ds(k0, bk)]
        for h in range(nh):
            raw = jnp.dot(q_ref[:, h * hw : (h + 1) * hw], kT, preferred_element_type=jnp.float32)
            s = raw * factor
            s = s - sg_ref[h] * dist + sg_ref[nh + h] * anc
            s = jnp.where(allowed, s, masked_score)
            s_scr[h, kb] = s
            m_old = m_scr[h]
            m_new = jnp.maximum(m_old, jnp.max(s, axis=1, keepdims=True))
            l_scr[h] = l_scr[h] * jnp.exp(m_old - m_new) + jnp.sum(
                jnp.exp(s - m_new), axis=1, keepdims=True
            )
            m_scr[h] = m_new
        return carry

    lax.fori_loop(lo, i + 1, stats, 0)
    for h in range(nh):
        m_scr[h] = m_scr[h] + jnp.log(l_scr[h])
    dq_scr[...] = jnp.zeros(dq_scr.shape, jnp.float32)

    def grads(kb, carry):
        k0, _, anc, dist = tile_masks(kb)
        vT = vT_ref[:, pl.ds(k0, bk)]
        kblk = k_ref[pl.ds(k0, bk), :]
        for h in range(nh):
            s = s_scr[h, kb]
            p = jnp.exp(s - m_scr[h])
            dp = jnp.dot(do_ref[:, h * hw : (h + 1) * hw], vT, preferred_element_type=jnp.float32)
            ds = p * (dp - delta_ref[:, h : h + 1])
            ds_b = ds.astype(jnp.bfloat16)
            p_b = p.astype(jnp.bfloat16)
            dq_scr[h] += jnp.dot(ds_b, kblk, preferred_element_type=jnp.float32)
            dkT_ref[:, pl.ds(k0, bk)] += jnp.dot(
                qT_ref[h * hw : (h + 1) * hw, :], ds_b, preferred_element_type=jnp.float32
            )
            dvT_ref[:, pl.ds(k0, bk)] += jnp.dot(
                doT_ref[h * hw : (h + 1) * hw, :], p_b, preferred_element_type=jnp.float32
            )
            bias_ref[h] += jnp.sum(ds * dist, axis=0, keepdims=True)
            bias_ref[nh + h] += jnp.sum(ds * anc, axis=0, keepdims=True)
        return carry

    lax.fori_loop(lo, i + 1, grads, 0)
    for h in range(nh):
        dq_ref[:, h * hw : (h + 1) * hw] = (dq_scr[h] * factor).astype(dq_ref.dtype)


def attention_grads(q, qT, do, doT, delta, k, kT, vT, dcol, fcol, drow, frow, erow, lo, sg, interpret=False):
    seq_len, width = q.shape
    hw = k.shape[1]
    nh = width // hw
    bq = bk = min(BLOCK, seq_len)
    nq = seq_len // bq
    nk = seq_len // bk
    factor = hw ** (-0.5)
    kernel = functools.partial(_grads_kernel, nh=nh, hw=hw, bq=bq, bk=bk, factor=factor)
    full = lambda shape: pl.BlockSpec(shape, lambda i, lo: (0,) * len(shape))
    grid_spec = pltpu.PrefetchScalarGridSpec(
        num_scalar_prefetch=1,
        grid=(nq,),
        in_specs=[
            pl.BlockSpec(memory_space=pltpu.SMEM),
            pl.BlockSpec((bq, width), lambda i, lo: (i, 0)),
            pl.BlockSpec((width, bq), lambda i, lo: (0, i)),
            pl.BlockSpec((bq, width), lambda i, lo: (i, 0)),
            pl.BlockSpec((width, bq), lambda i, lo: (0, i)),
            pl.BlockSpec((bq, nh), lambda i, lo: (i, 0)),
            full((seq_len, hw)),
            full((hw, seq_len)),
            full((hw, seq_len)),
            pl.BlockSpec((bq, 1), lambda i, lo: (i, 0)),
            pl.BlockSpec((bq, 1), lambda i, lo: (i, 0)),
            full((1, seq_len)),
            full((1, seq_len)),
            full((1, seq_len)),
        ],
        out_specs=[
            pl.BlockSpec((bq, width), lambda i, lo: (i, 0)),
            full((hw, seq_len)),
            full((hw, seq_len)),
            full((2 * nh, 1, bk)),
        ],
        scratch_shapes=[
            pltpu.VMEM((nh, nk, bq, bk), jnp.float32),
            pltpu.VMEM((nh, bq, 1), jnp.float32),
            pltpu.VMEM((nh, bq, 1), jnp.float32),
            pltpu.VMEM((nh, bq, hw), jnp.float32),
        ],
    )
    causal_tiles = nq * (nq + 1) // 2
    flops = 2 * 5 * nh * causal_tiles * bq * bk * hw
    return pl.pallas_call(
        kernel,
        grid_spec=grid_spec,
        out_shape=[
            jax.ShapeDtypeStruct((seq_len, width), jnp.bfloat16),
            jax.ShapeDtypeStruct((hw, seq_len), jnp.float32),
            jax.ShapeDtypeStruct((hw, seq_len), jnp.float32),
            jax.ShapeDtypeStruct((2 * nh, 1, bk), jnp.float32),
        ],
        compiler_params=pltpu.CompilerParams(
            dimension_semantics=("arbitrary",), vmem_limit_bytes=48 * 1024 * 1024
        ),
        cost_estimate=pl.CostEstimate(
            flops=flops,
            transcendentals=2 * nh * causal_tiles * bq * bk,
            bytes_accessed=8 * seq_len * width + 8 * seq_len * hw,
        ),
        interpret=interpret,
    )(lo, sg, q, qT, do, doT, delta, k, kT, vT, dcol, fcol, drow, frow, erow)


def body(
    queries,
    key_rows,
    values,
    outputs,
    out_grads,
    depths,
    subtree_end,
    file_lengths,
    slopes,
    ancestor_gain,
):
    tokens_here = queries.shape[1]
    context_size = lax.axis_size("ctx")
    heads_all = queries.shape[2] // HEAD_WIDTH
    kv_heads = key_rows.shape[2] // HEAD_WIDTH
    local_heads = heads_all // context_size
    group_width = heads_all // kv_heads
    repeats = context_size // kv_heads
    assert group_width // local_heads == repeats
    seq_len = tokens_here * context_size
    block = min(BLOCK, seq_len)
    factor = HEAD_WIDTH ** (-0.5)
    head_first = lax.axis_index("ctx") * local_heads
    local_slopes = lax.dynamic_slice_in_dim(slopes, head_first, local_heads)
    local_gains = lax.dynamic_slice_in_dim(ancestor_gain, head_first, local_heads)
    sg = jnp.concatenate([local_slopes, local_gains])
    positions = jnp.arange(seq_len, dtype=jnp.int32)
    lengths = file_lengths[0]
    bounds = jnp.cumsum(lengths)
    starts = bounds - lengths
    file_whole = jnp.sum((positions[:, None] >= bounds[None, :]).astype(jnp.int32), axis=1)
    file_start = starts[jnp.minimum(file_whole, lengths.shape[0] - 1)]
    lo = (file_start[::block] // block).astype(jnp.int32)

    delta_tok = jnp.sum(
        (out_grads[0].astype(jnp.float32) * outputs[0].astype(jnp.float32)).reshape(
            tokens_here, heads_all, HEAD_WIDTH
        ),
        axis=2,
    )
    tree_tok = jnp.stack([depths[0], subtree_end[0]], axis=1).astype(jnp.float32)
    small_pack = jnp.concatenate(
        [
            delta_tok.reshape(tokens_here, context_size, local_heads),
            jnp.broadcast_to(tree_tok[:, None, :], (tokens_here, context_size, 2)),
        ],
        axis=2,
    )
    small_heads = lax.all_to_all(small_pack, "ctx", split_axis=1, concat_axis=0, tiled=True).reshape(
        seq_len, local_heads + 2
    )
    delta_heads = small_heads[:, :local_heads]
    depth_whole = small_heads[:, local_heads].astype(jnp.int32)
    end_whole = small_heads[:, local_heads + 1].astype(jnp.int32)

    width = local_heads * HEAD_WIDTH
    big_pack = jnp.concatenate(
        [
            queries[0].reshape(tokens_here, context_size, width),
            out_grads[0].reshape(tokens_here, context_size, width),
            jnp.repeat(key_rows[0].reshape(tokens_here, kv_heads, HEAD_WIDTH), repeats, axis=1),
            jnp.repeat(values[0].reshape(tokens_here, kv_heads, HEAD_WIDTH), repeats, axis=1),
        ],
        axis=2,
    )
    big_heads = lax.all_to_all(big_pack, "ctx", split_axis=1, concat_axis=0, tiled=True).reshape(
        seq_len, 2 * width + 2 * HEAD_WIDTH
    )
    query_heads = big_heads[:, :width]
    grad_heads = big_heads[:, width : 2 * width]
    key_head = big_heads[:, 2 * width : 2 * width + HEAD_WIDTH]
    value_head = big_heads[:, 2 * width + HEAD_WIDTH :]

    dq, dkT, dvT, bias_part = attention_grads(
        query_heads,
        query_heads.T,
        grad_heads,
        grad_heads.T,
        delta_heads,
        key_head,
        key_head.T,
        value_head.T,
        depth_whole[:, None],
        file_whole[:, None],
        depth_whole[None, :],
        file_whole[None, :],
        end_whole[None, :],
        lo,
        sg,
    )

    back_pack = jnp.concatenate(
        [dq, (dkT.T * factor).astype(jnp.bfloat16), dvT.T.astype(jnp.bfloat16)], axis=1
    ).reshape(seq_len, 1, width + 2 * HEAD_WIDTH)
    back = lax.all_to_all(back_pack, "ctx", split_axis=0, concat_axis=1, tiled=True)
    query_grads = back[:, :, :width].reshape(1, tokens_here, heads_all * HEAD_WIDTH)
    key_back = back[:, :, width : width + HEAD_WIDTH].astype(jnp.float32)
    value_back = back[:, :, width + HEAD_WIDTH :].astype(jnp.float32)
    key_grads = jnp.sum(key_back.reshape(tokens_here, kv_heads, repeats, HEAD_WIDTH), axis=2)
    value_grads = jnp.sum(value_back.reshape(tokens_here, kv_heads, repeats, HEAD_WIDTH), axis=2)
    key_grads = key_grads.astype(jnp.bfloat16).reshape(1, tokens_here, kv_heads * HEAD_WIDTH)
    value_grads = value_grads.astype(jnp.bfloat16).reshape(1, tokens_here, kv_heads * HEAD_WIDTH)
    bias_sums = jnp.sum(bias_part, axis=(1, 2))
    bias_local = jnp.stack([-bias_sums[:local_heads], bias_sums[local_heads:]], axis=1)
    data_size = lax.axis_size("dp")
    bias_copies = jnp.broadcast_to(bias_local[None], (data_size, local_heads, 2))
    bias_each = lax.all_to_all(bias_copies, "dp", split_axis=0, concat_axis=0, tiled=True)
    bias_grads = jnp.sum(bias_each, axis=0)
    return (query_grads, key_grads, value_grads, bias_grads)


def solution(mesh):
    in_specs = (
        P("dp", "ctx", None),
        P("dp", "ctx", None),
        P("dp", "ctx", None),
        P("dp", "ctx", None),
        P("dp", "ctx", None),
        P("dp", "ctx"),
        P("dp", "ctx"),
        P("dp", None),
        P(),
        P(),
    )
    out_specs = (P("dp", "ctx", None), P("dp", "ctx", None), P("dp", "ctx", None), P("ctx", None))
    return jax.shard_map(body, mesh=mesh, in_specs=in_specs, out_specs=out_specs, check_vma=False)
```

```python
import functools

import jax
import jax.numpy as jnp
from jax import lax
from jax.experimental import pallas as pl
from jax.experimental.pallas import tpu as pltpu
from jax.sharding import PartitionSpec as P

HEAD_WIDTH = 128
BLOCK = 256

masked_score = -1e30


def _grads_kernel(
    lo_ref,
    sg_ref,
    q_ref,
    do_ref,
    small_ref,
    k_ref,
    v_ref,
    dcol_ref,
    fcol_ref,
    drow_ref,
    frow_ref,
    erow_ref,
    *rest,
    hw,
    bq,
    bk,
    factor,
    head,
    accumulate,
):
    if accumulate:
        dkT_in, dvT_in = rest[:2]
        rest = rest[2:]
    dq_ref, dkT_ref, dvT_ref, bias_ref, s_scr, m_scr, l_scr, dq_scr, qT_scr, doT_scr = rest
    i = pl.program_id(0)

    @pl.when(i == 0)
    def _():
        if accumulate:
            dkT_ref[...] = dkT_in[...]
            dvT_ref[...] = dvT_in[...]
        else:
            dkT_ref[...] = jnp.zeros_like(dkT_ref)
            dvT_ref[...] = jnp.zeros_like(dvT_ref)
        bias_ref[...] = jnp.zeros_like(bias_ref)

    q0 = i * bq
    lo = lo_ref[i]
    qpos = q0 + lax.broadcasted_iota(jnp.int32, (bq, 1), 0)
    dcol = dcol_ref[...]
    fcol = fcol_ref[...]
    slope = sg_ref[0]
    gain = sg_ref[1]
    nt = (((1,), (1,)), ((), ()))

    def tile_masks(kb):
        k0 = pl.multiple_of(kb * bk, bk)
        kpos = k0 + lax.broadcasted_iota(jnp.int32, (1, bk), 1)
        drow = drow_ref[:, pl.ds(k0, bk)]
        frow = frow_ref[:, pl.ds(k0, bk)]
        erow = erow_ref[:, pl.ds(k0, bk)]
        causal = kpos <= qpos
        allowed = causal & (fcol == frow)
        anc = jnp.where(causal & (qpos < erow), 1.0, 0.0).astype(jnp.float32)
        dist = jnp.abs(dcol - drow).astype(jnp.float32)
        return k0, allowed, anc, dist

    m_scr[...] = jnp.full(m_scr.shape, masked_score, jnp.float32)
    l_scr[...] = jnp.zeros(l_scr.shape, jnp.float32)
    qT_scr[...] = q_ref[...].astype(jnp.float32).T.astype(qT_scr.dtype)
    doT_scr[...] = do_ref[...].astype(jnp.float32).T.astype(doT_scr.dtype)

    def stats(kb, carry):
        k0, allowed, anc, dist = tile_masks(kb)
        raw = lax.dot_general(q_ref[...], k_ref[pl.ds(k0, bk), :], nt, preferred_element_type=jnp.float32)
        s = raw * factor
        s = s - slope * dist + gain * anc
        s = jnp.where(allowed, s, masked_score)
        s_scr[kb] = s
        m_old = m_scr[...]
        m_new = jnp.maximum(m_old, jnp.max(s, axis=1, keepdims=True))
        l_scr[...] = l_scr[...] * jnp.exp(m_old - m_new) + jnp.sum(jnp.exp(s - m_new), axis=1, keepdims=True)
        m_scr[...] = m_new
        return carry

    lax.fori_loop(lo, i + 1, stats, 0)
    m_scr[...] = m_scr[...] + jnp.log(l_scr[...])
    dq_scr[...] = jnp.zeros(dq_scr.shape, jnp.float32)

    def grads(kb, carry):
        k0, _, anc, dist = tile_masks(kb)
        s = s_scr[kb]
        p = jnp.exp(s - m_scr[...])
        dp = lax.dot_general(do_ref[...], v_ref[pl.ds(k0, bk), :], nt, preferred_element_type=jnp.float32)
        ds = p * (dp - small_ref[:, head : head + 1])
        ds_b = ds.astype(jnp.bfloat16)
        p_b = p.astype(jnp.bfloat16)
        dq_scr[...] += jnp.dot(ds_b, k_ref[pl.ds(k0, bk), :], preferred_element_type=jnp.float32)
        dkT_ref[:, pl.ds(k0, bk)] += jnp.dot(qT_scr[...], ds_b, preferred_element_type=jnp.float32)
        dvT_ref[:, pl.ds(k0, bk)] += jnp.dot(doT_scr[...], p_b, preferred_element_type=jnp.float32)
        bias_ref[0] += jnp.sum(ds * dist, axis=0, keepdims=True)
        bias_ref[1] += jnp.sum(ds * anc, axis=0, keepdims=True)
        return carry

    lax.fori_loop(lo, i + 1, grads, 0)
    dq_ref[...] = (dq_scr[...] * factor).astype(dq_ref.dtype)


def attention_grads(
    x, q_col, do_col, kv, k_col, v_col, small, head, dcol, fcol, drow, frow, erow, lo, sg, acc=None, interpret=False
):
    seq_len, hw = kv.shape[0], HEAD_WIDTH
    bq = bk = min(BLOCK, seq_len)
    nq = seq_len // bq
    nk = seq_len // bk
    factor = hw ** (-0.5)
    accumulate = acc is not None
    kernel = functools.partial(
        _grads_kernel, hw=hw, bq=bq, bk=bk, factor=factor, head=head, accumulate=accumulate
    )
    full = lambda shape: pl.BlockSpec(shape, lambda i, lo: (0,) * len(shape))
    in_specs = [
        pl.BlockSpec(memory_space=pltpu.SMEM),
        pl.BlockSpec((bq, hw), lambda i, lo: (i, q_col)),
        pl.BlockSpec((bq, hw), lambda i, lo: (i, do_col)),
        pl.BlockSpec((bq, small.shape[1]), lambda i, lo: (i, 0)),
        pl.BlockSpec((seq_len, hw), lambda i, lo: (0, k_col)),
        pl.BlockSpec((seq_len, hw), lambda i, lo: (0, v_col)),
        pl.BlockSpec((bq, 1), lambda i, lo: (i, 0)),
        pl.BlockSpec((bq, 1), lambda i, lo: (i, 0)),
        full((1, seq_len)),
        full((1, seq_len)),
        full((1, seq_len)),
    ]
    args = [lo, sg, x, x, small, kv, kv, dcol, fcol, drow, frow, erow]
    if accumulate:
        in_specs += [full((hw, seq_len)), full((hw, seq_len))]
        args += list(acc)
    grid_spec = pltpu.PrefetchScalarGridSpec(
        num_scalar_prefetch=1,
        grid=(nq,),
        in_specs=in_specs,
        out_specs=[
            pl.BlockSpec((bq, hw), lambda i, lo: (i, 0)),
            full((hw, seq_len)),
            full((hw, seq_len)),
            full((2, 1, bk)),
        ],
        scratch_shapes=[
            pltpu.VMEM((nk, bq, bk), jnp.float32),
            pltpu.VMEM((bq, 1), jnp.float32),
            pltpu.VMEM((bq, 1), jnp.float32),
            pltpu.VMEM((bq, hw), jnp.float32),
            pltpu.VMEM((hw, bq), jnp.bfloat16),
            pltpu.VMEM((hw, bq), jnp.bfloat16),
        ],
    )
    causal_tiles = nq * (nq + 1) // 2
    flops = 2 * 5 * causal_tiles * bq * bk * hw
    return pl.pallas_call(
        kernel,
        grid_spec=grid_spec,
        out_shape=[
            jax.ShapeDtypeStruct((seq_len, hw), jnp.bfloat16),
            jax.ShapeDtypeStruct((hw, seq_len), jnp.float32),
            jax.ShapeDtypeStruct((hw, seq_len), jnp.float32),
            jax.ShapeDtypeStruct((2, 1, bk), jnp.float32),
        ],
        compiler_params=pltpu.CompilerParams(
            dimension_semantics=("arbitrary",), vmem_limit_bytes=48 * 1024 * 1024
        ),
        cost_estimate=pl.CostEstimate(
            flops=flops,
            transcendentals=2 * causal_tiles * bq * bk,
            bytes_accessed=8 * seq_len * hw,
        ),
        interpret=interpret,
    )(*args)


def body(
    queries,
    key_rows,
    values,
    outputs,
    out_grads,
    depths,
    subtree_end,
    file_lengths,
    slopes,
    ancestor_gain,
):
    tokens_here = queries.shape[1]
    context_size = lax.axis_size("ctx")
    heads_all = queries.shape[2] // HEAD_WIDTH
    kv_heads = key_rows.shape[2] // HEAD_WIDTH
    local_heads = heads_all // context_size
    group_width = heads_all // kv_heads
    repeats = context_size // kv_heads
    assert group_width // local_heads == repeats
    seq_len = tokens_here * context_size
    block = min(BLOCK, seq_len)
    factor = HEAD_WIDTH ** (-0.5)
    head_first = lax.axis_index("ctx") * local_heads
    local_slopes = lax.dynamic_slice_in_dim(slopes, head_first, local_heads)
    local_gains = lax.dynamic_slice_in_dim(ancestor_gain, head_first, local_heads)
    positions = jnp.arange(seq_len, dtype=jnp.int32)
    lengths = file_lengths[0]
    bounds = jnp.cumsum(lengths)
    starts = bounds - lengths
    file_whole = jnp.sum((positions[:, None] >= bounds[None, :]).astype(jnp.int32), axis=1)
    file_start = starts[jnp.minimum(file_whole, lengths.shape[0] - 1)]
    lo = (file_start[::block] // block).astype(jnp.int32)

    delta_tok = jnp.sum(
        (out_grads[0].astype(jnp.float32) * outputs[0].astype(jnp.float32)).reshape(
            tokens_here, heads_all, HEAD_WIDTH
        ),
        axis=2,
    )
    tree_tok = jnp.stack([depths[0], subtree_end[0]], axis=1).astype(jnp.float32)
    small_pack = jnp.concatenate(
        [
            delta_tok.reshape(tokens_here, context_size, local_heads),
            jnp.broadcast_to(tree_tok[:, None, :], (tokens_here, context_size, 2)),
        ],
        axis=2,
    )
    small_heads = lax.all_to_all(small_pack, "ctx", split_axis=1, concat_axis=0, tiled=True).reshape(
        seq_len, local_heads + 2
    )
    depth_whole = small_heads[:, local_heads].astype(jnp.int32)
    end_whole = small_heads[:, local_heads + 1].astype(jnp.int32)

    width = local_heads * HEAD_WIDTH
    query_split = queries[0].reshape(tokens_here, context_size, local_heads, HEAD_WIDTH)
    grad_split = out_grads[0].reshape(tokens_here, context_size, local_heads, HEAD_WIDTH)
    key_rep = jnp.repeat(key_rows[0].reshape(tokens_here, kv_heads, HEAD_WIDTH), repeats, axis=1)
    value_rep = jnp.repeat(values[0].reshape(tokens_here, kv_heads, HEAD_WIDTH), repeats, axis=1)
    chunks = []
    for h in range(local_heads):
        parts = [query_split[:, :, h], grad_split[:, :, h]]
        if h == 0:
            parts += [key_rep, value_rep]
        pack = jnp.concatenate(parts, axis=2)
        got = lax.all_to_all(pack, "ctx", split_axis=1, concat_axis=0, tiled=True)
        chunks.append(got.reshape(seq_len, pack.shape[2]))
    kv = chunks[0]
    tree = (
        depth_whole[:, None],
        file_whole[:, None],
        depth_whole[None, :],
        file_whole[None, :],
        end_whole[None, :],
        lo,
    )
    acc = None
    dq_back = []
    bias_rows = []
    for h in range(local_heads):
        sg = jnp.stack([local_slopes[h], local_gains[h]])
        dq_h, dkT, dvT, bias_part = attention_grads(
            chunks[h], 0, 1, kv, 2, 3, small_heads, h, *tree, sg, acc=acc
        )
        acc = (dkT, dvT)
        bias_sums = jnp.sum(bias_part, axis=(1, 2))
        bias_rows.append(jnp.stack([-bias_sums[0], bias_sums[1]]))
        if h < local_heads - 1:
            back_h = lax.all_to_all(
                dq_h.reshape(seq_len, 1, HEAD_WIDTH), "ctx", split_axis=0, concat_axis=1, tiled=True
            )
            dq_back.append(back_h)
    back_pack = jnp.concatenate(
        [dq_h, (dkT.T * factor).astype(jnp.bfloat16), dvT.T.astype(jnp.bfloat16)], axis=1
    ).reshape(seq_len, 1, 3 * HEAD_WIDTH)
    back = lax.all_to_all(back_pack, "ctx", split_axis=0, concat_axis=1, tiled=True)
    dq_back.append(back[:, :, :HEAD_WIDTH])
    query_grads = jnp.stack(dq_back, axis=2).reshape(1, tokens_here, heads_all * HEAD_WIDTH)
    key_back = back[:, :, HEAD_WIDTH : 2 * HEAD_WIDTH].astype(jnp.float32)
    value_back = back[:, :, 2 * HEAD_WIDTH :].astype(jnp.float32)
    key_grads = jnp.sum(key_back.reshape(tokens_here, kv_heads, repeats, HEAD_WIDTH), axis=2)
    value_grads = jnp.sum(value_back.reshape(tokens_here, kv_heads, repeats, HEAD_WIDTH), axis=2)
    key_grads = key_grads.astype(jnp.bfloat16).reshape(1, tokens_here, kv_heads * HEAD_WIDTH)
    value_grads = value_grads.astype(jnp.bfloat16).reshape(1, tokens_here, kv_heads * HEAD_WIDTH)
    bias_local = jnp.stack(bias_rows, axis=0)
    data_size = lax.axis_size("dp")
    bias_copies = jnp.broadcast_to(bias_local[None], (data_size, local_heads, 2))
    bias_each = lax.all_to_all(bias_copies, "dp", split_axis=0, concat_axis=0, tiled=True)
    bias_grads = jnp.sum(bias_each, axis=0)
    return (query_grads, key_grads, value_grads, bias_grads)


def solution(mesh):
    in_specs = (
        P("dp", "ctx", None),
        P("dp", "ctx", None),
        P("dp", "ctx", None),
        P("dp", "ctx", None),
        P("dp", "ctx", None),
        P("dp", "ctx"),
        P("dp", "ctx"),
        P("dp", None),
        P(),
        P(),
    )
    out_specs = (P("dp", "ctx", None), P("dp", "ctx", None), P("dp", "ctx", None), P("ctx", None))
    return jax.shard_map(body, mesh=mesh, in_specs=in_specs, out_specs=out_specs, check_vma=False)
```

```python
import functools

import jax
import jax.numpy as jnp
from jax import lax
from jax.experimental import pallas as pl
from jax.experimental.pallas import tpu as pltpu
from jax.sharding import PartitionSpec as P

HEAD_WIDTH = 128
BLOCK = 256

masked_score = -1e30


def _grads_kernel(
    lo_ref,
    sg_ref,
    q_ref,
    qT_ref,
    do_ref,
    doT_ref,
    delta_ref,
    k_ref,
    kT_ref,
    vT_ref,
    dcol_ref,
    fcol_ref,
    drow_ref,
    frow_ref,
    erow_ref,
    dq_ref,
    dkT_ref,
    dvT_ref,
    bias_ref,
    s_scr,
    m_scr,
    l_scr,
    dq_scr,
    *,
    nh,
    hw,
    bq,
    bk,
    factor,
):
    i = pl.program_id(0)

    @pl.when(i == 0)
    def _():
        dkT_ref[...] = jnp.zeros_like(dkT_ref)
        dvT_ref[...] = jnp.zeros_like(dvT_ref)
        bias_ref[...] = jnp.zeros_like(bias_ref)

    q0 = i * bq
    lo = lo_ref[i]
    qpos = q0 + lax.broadcasted_iota(jnp.int32, (bq, 1), 0)
    dcol = dcol_ref[...]
    fcol = fcol_ref[...]

    def tile_masks(kb):
        k0 = pl.multiple_of(kb * bk, bk)
        kpos = k0 + lax.broadcasted_iota(jnp.int32, (1, bk), 1)
        drow = drow_ref[:, pl.ds(k0, bk)]
        frow = frow_ref[:, pl.ds(k0, bk)]
        erow = erow_ref[:, pl.ds(k0, bk)]
        causal = kpos <= qpos
        allowed = causal & (fcol == frow)
        anc = jnp.where(causal & (qpos < erow), 1.0, 0.0).astype(jnp.float32)
        dist = jnp.abs(dcol - drow).astype(jnp.float32)
        return k0, allowed, anc, dist

    m_scr[...] = jnp.full(m_scr.shape, masked_score, jnp.float32)
    l_scr[...] = jnp.zeros(l_scr.shape, jnp.float32)

    def stats(kb, carry):
        k0, allowed, anc, dist = tile_masks(kb)
        kT = kT_ref[:, pl.ds(k0, bk)]
        for h in range(nh):
            raw = jnp.dot(q_ref[:, h * hw : (h + 1) * hw], kT, preferred_element_type=jnp.float32)
            s = raw * factor
            s = s - sg_ref[h] * dist + sg_ref[nh + h] * anc
            s = jnp.where(allowed, s, masked_score)
            s_scr[h, kb] = s
            m_old = m_scr[h]
            m_new = jnp.maximum(m_old, jnp.max(s, axis=1, keepdims=True))
            l_scr[h] = l_scr[h] * jnp.exp(m_old - m_new) + jnp.sum(
                jnp.exp(s - m_new), axis=1, keepdims=True
            )
            m_scr[h] = m_new
        return carry

    lax.fori_loop(lo, i + 1, stats, 0)
    for h in range(nh):
        m_scr[h] = m_scr[h] + jnp.log(l_scr[h])
    dq_scr[...] = jnp.zeros(dq_scr.shape, jnp.float32)

    def grads(kb, carry):
        k0, _, anc, dist = tile_masks(kb)
        vT = vT_ref[:, pl.ds(k0, bk)]
        kblk = k_ref[pl.ds(k0, bk), :]
        for h in range(nh):
            s = s_scr[h, kb]
            p = jnp.exp(s - m_scr[h])
            dp = jnp.dot(do_ref[:, h * hw : (h + 1) * hw], vT, preferred_element_type=jnp.float32)
            ds = p * (dp - delta_ref[:, h : h + 1])
            ds_b = ds.astype(jnp.bfloat16)
            p_b = p.astype(jnp.bfloat16)
            dq_scr[h] += jnp.dot(ds_b, kblk, preferred_element_type=jnp.float32)
            dkT_ref[:, pl.ds(k0, bk)] += jnp.dot(
                qT_ref[h * hw : (h + 1) * hw, :], ds_b, preferred_element_type=jnp.float32
            )
            dvT_ref[:, pl.ds(k0, bk)] += jnp.dot(
                doT_ref[h * hw : (h + 1) * hw, :], p_b, preferred_element_type=jnp.float32
            )
            bias_ref[h] += jnp.sum(ds * dist, axis=0, keepdims=True)
            bias_ref[nh + h] += jnp.sum(ds * anc, axis=0, keepdims=True)
        return carry

    lax.fori_loop(lo, i + 1, grads, 0)
    for h in range(nh):
        dq_ref[:, h * hw : (h + 1) * hw] = (dq_scr[h] * factor).astype(dq_ref.dtype)


def attention_grads(x, xT, nh, delta, dcol, fcol, drow, frow, erow, lo, sg, interpret=False):
    seq_len = x.shape[0]
    hw = HEAD_WIDTH
    width = nh * hw
    k_col = 2 * nh
    bq = bk = min(BLOCK, seq_len)
    nq = seq_len // bq
    nk = seq_len // bk
    factor = hw ** (-0.5)
    kernel = functools.partial(_grads_kernel, nh=nh, hw=hw, bq=bq, bk=bk, factor=factor)
    full = lambda shape: pl.BlockSpec(shape, lambda i, lo: (0,) * len(shape))
    grid_spec = pltpu.PrefetchScalarGridSpec(
        num_scalar_prefetch=1,
        grid=(nq,),
        in_specs=[
            pl.BlockSpec(memory_space=pltpu.SMEM),
            pl.BlockSpec((bq, width), lambda i, lo: (i, 0)),
            pl.BlockSpec((width, bq), lambda i, lo: (0, i)),
            pl.BlockSpec((bq, width), lambda i, lo: (i, 1)),
            pl.BlockSpec((width, bq), lambda i, lo: (1, i)),
            pl.BlockSpec((bq, nh), lambda i, lo: (i, 0)),
            pl.BlockSpec((seq_len, hw), lambda i, lo: (0, k_col)),
            pl.BlockSpec((hw, seq_len), lambda i, lo: (k_col, 0)),
            pl.BlockSpec((hw, seq_len), lambda i, lo: (k_col + 1, 0)),
            pl.BlockSpec((bq, 1), lambda i, lo: (i, 0)),
            pl.BlockSpec((bq, 1), lambda i, lo: (i, 0)),
            full((1, seq_len)),
            full((1, seq_len)),
            full((1, seq_len)),
        ],
        out_specs=[
            pl.BlockSpec((bq, width), lambda i, lo: (i, 0)),
            full((hw, seq_len)),
            full((hw, seq_len)),
            full((2 * nh, 1, bk)),
        ],
        scratch_shapes=[
            pltpu.VMEM((nh, nk, bq, bk), jnp.float32),
            pltpu.VMEM((nh, bq, 1), jnp.float32),
            pltpu.VMEM((nh, bq, 1), jnp.float32),
            pltpu.VMEM((nh, bq, hw), jnp.float32),
        ],
    )
    causal_tiles = nq * (nq + 1) // 2
    flops = 2 * 5 * nh * causal_tiles * bq * bk * hw
    return pl.pallas_call(
        kernel,
        grid_spec=grid_spec,
        out_shape=[
            jax.ShapeDtypeStruct((seq_len, width), jnp.bfloat16),
            jax.ShapeDtypeStruct((hw, seq_len), jnp.float32),
            jax.ShapeDtypeStruct((hw, seq_len), jnp.float32),
            jax.ShapeDtypeStruct((2 * nh, 1, bk), jnp.float32),
        ],
        compiler_params=pltpu.CompilerParams(
            dimension_semantics=("arbitrary",), vmem_limit_bytes=48 * 1024 * 1024
        ),
        cost_estimate=pl.CostEstimate(
            flops=flops,
            transcendentals=2 * nh * causal_tiles * bq * bk,
            bytes_accessed=8 * seq_len * width + 8 * seq_len * hw,
        ),
        interpret=interpret,
    )(lo, sg, x, xT, x, xT, delta, x, xT, xT, dcol, fcol, drow, frow, erow)


def body(
    queries,
    key_rows,
    values,
    outputs,
    out_grads,
    depths,
    subtree_end,
    file_lengths,
    slopes,
    ancestor_gain,
):
    tokens_here = queries.shape[1]
    context_size = lax.axis_size("ctx")
    heads_all = queries.shape[2] // HEAD_WIDTH
    kv_heads = key_rows.shape[2] // HEAD_WIDTH
    local_heads = heads_all // context_size
    group_width = heads_all // kv_heads
    repeats = context_size // kv_heads
    assert group_width // local_heads == repeats
    seq_len = tokens_here * context_size
    block = min(BLOCK, seq_len)
    factor = HEAD_WIDTH ** (-0.5)
    head_first = lax.axis_index("ctx") * local_heads
    local_slopes = lax.dynamic_slice_in_dim(slopes, head_first, local_heads)
    local_gains = lax.dynamic_slice_in_dim(ancestor_gain, head_first, local_heads)
    sg = jnp.concatenate([local_slopes, local_gains])
    positions = jnp.arange(seq_len, dtype=jnp.int32)
    lengths = file_lengths[0]
    bounds = jnp.cumsum(lengths)
    starts = bounds - lengths
    file_whole = jnp.sum((positions[:, None] >= bounds[None, :]).astype(jnp.int32), axis=1)
    file_start = starts[jnp.minimum(file_whole, lengths.shape[0] - 1)]
    lo = (file_start[::block] // block).astype(jnp.int32)

    delta_tok = jnp.sum(
        (out_grads[0].astype(jnp.float32) * outputs[0].astype(jnp.float32)).reshape(
            tokens_here, heads_all, HEAD_WIDTH
        ),
        axis=2,
    )
    tree_tok = jnp.stack([depths[0], subtree_end[0]], axis=1).astype(jnp.float32)
    small_pack = jnp.concatenate(
        [
            delta_tok.reshape(tokens_here, context_size, local_heads),
            jnp.broadcast_to(tree_tok[:, None, :], (tokens_here, context_size, 2)),
        ],
        axis=2,
    )
    small_heads = lax.all_to_all(small_pack, "ctx", split_axis=1, concat_axis=0, tiled=True).reshape(
        seq_len, local_heads + 2
    )
    delta_heads = small_heads[:, :local_heads]
    depth_whole = small_heads[:, local_heads].astype(jnp.int32)
    end_whole = small_heads[:, local_heads + 1].astype(jnp.int32)

    width = local_heads * HEAD_WIDTH
    big_pack = jnp.concatenate(
        [
            queries[0].reshape(tokens_here, context_size, width),
            out_grads[0].reshape(tokens_here, context_size, width),
            jnp.repeat(key_rows[0].reshape(tokens_here, kv_heads, HEAD_WIDTH), repeats, axis=1),
            jnp.repeat(values[0].reshape(tokens_here, kv_heads, HEAD_WIDTH), repeats, axis=1),
        ],
        axis=2,
    )
    big_heads = lax.all_to_all(big_pack, "ctx", split_axis=1, concat_axis=0, tiled=True).reshape(
        seq_len, 2 * width + 2 * HEAD_WIDTH
    )

    dq, dkT, dvT, bias_part = attention_grads(
        big_heads,
        big_heads.T,
        local_heads,
        delta_heads,
        depth_whole[:, None],
        file_whole[:, None],
        depth_whole[None, :],
        file_whole[None, :],
        end_whole[None, :],
        lo,
        sg,
    )

    back_pack = jnp.concatenate(
        [dq, (dkT.T * factor).astype(jnp.bfloat16), dvT.T.astype(jnp.bfloat16)], axis=1
    ).reshape(seq_len, 1, width + 2 * HEAD_WIDTH)
    back = lax.all_to_all(back_pack, "ctx", split_axis=0, concat_axis=1, tiled=True)
    query_grads = back[:, :, :width].reshape(1, tokens_here, heads_all * HEAD_WIDTH)
    key_back = back[:, :, width : width + HEAD_WIDTH].astype(jnp.float32)
    value_back = back[:, :, width + HEAD_WIDTH :].astype(jnp.float32)
    key_grads = jnp.sum(key_back.reshape(tokens_here, kv_heads, repeats, HEAD_WIDTH), axis=2)
    value_grads = jnp.sum(value_back.reshape(tokens_here, kv_heads, repeats, HEAD_WIDTH), axis=2)
    key_grads = key_grads.astype(jnp.bfloat16).reshape(1, tokens_here, kv_heads * HEAD_WIDTH)
    value_grads = value_grads.astype(jnp.bfloat16).reshape(1, tokens_here, kv_heads * HEAD_WIDTH)
    bias_sums = jnp.sum(bias_part, axis=(1, 2))
    bias_local = jnp.stack([-bias_sums[:local_heads], bias_sums[local_heads:]], axis=1)
    data_size = lax.axis_size("dp")
    bias_copies = jnp.broadcast_to(bias_local[None], (data_size, local_heads, 2))
    bias_each = lax.all_to_all(bias_copies, "dp", split_axis=0, concat_axis=0, tiled=True)
    bias_grads = jnp.sum(bias_each, axis=0)
    return (query_grads, key_grads, value_grads, bias_grads)


def solution(mesh):
    in_specs = (
        P("dp", "ctx", None),
        P("dp", "ctx", None),
        P("dp", "ctx", None),
        P("dp", "ctx", None),
        P("dp", "ctx", None),
        P("dp", "ctx"),
        P("dp", "ctx"),
        P("dp", None),
        P(),
        P(),
    )
    out_specs = (P("dp", "ctx", None), P("dp", "ctx", None), P("dp", "ctx", None), P("ctx", None))
    return jax.shard_map(body, mesh=mesh, in_specs=in_specs, out_specs=out_specs, check_vma=False)
```
